32 devices in a mesh: parts: 2 (over y), mp: 4 (over z), split: 4 (over x, core).
Axes of the slice: x: 2, y: 2, z: 4, core: 2. Of those that a mesh axis runs over, the one named last changes fastest.
Arguments:
- tokens: bfloat16 [384, 5120], P(('parts', 'mp'), 'split'), parts along dimension 0, may hold values from -6 to 6
- lengths: int32 [6], P('parts'), parts along dimension 0, may hold values from 1 to 64
- teacher_gate: bfloat16 [10240, 13824], P(('parts', 'split'), 'mp'), parts along dimension 0, may hold values from -0.078125 to 0.078125
- teacher_up: bfloat16 [10240, 13824], P(('parts', 'split'), 'mp'), parts along dimension 0, may hold values from -0.078125 to 0.078125
- teacher_down: bfloat16 [27648, 5120], P(('parts', 'mp'), 'split'), parts along dimension 0, may hold values from -0.0546875 to 0.0546875
- first_gate: bfloat16 [10240, 6912], P(('parts', 'split'), 'mp'), parts along dimension 0, may hold values from -0.078125 to 0.078125
- first_up: bfloat16 [10240, 6912], P(('parts', 'split'), 'mp'), parts along dimension 0, may hold values from -0.078125 to 0.078125
- first_down: bfloat16 [13824, 5120], P(('parts', 'mp'), 'split'), parts along dimension 0, may hold values from -0.078125 to 0.078125
- second_gate: bfloat16 [10240, 5632], P(('parts', 'split'), 'mp'), parts along dimension 0, may hold values from -0.078125 to 0.078125
- second_up: bfloat16 [10240, 5632], P(('parts', 'split'), 'mp'), parts along dimension 0, may hold values from -0.078125 to 0.078125
- second_down: bfloat16 [11264, 5120], P(('parts', 'mp'), 'split'), parts along dimension 0, may hold values from -0.078125 to 0.078125
Outputs:
- grad_first_gate: bfloat16 [10240, 6912], P(('parts', 'split'), 'mp'), parts along dimension 0
- grad_first_up: bfloat16 [10240, 6912], P(('parts', 'split'), 'mp'), parts along dimension 0
- grad_first_down: bfloat16 [13824, 5120], P(('parts', 'mp'), 'split'), parts along dimension 0
- grad_second_gate: bfloat16 [10240, 5632], P(('parts', 'split'), 'mp'), parts along dimension 0
- grad_second_up: bfloat16 [10240, 5632], P(('parts', 'split'), 'mp'), parts along dimension 0
- grad_second_down: bfloat16 [11264, 5120], P(('parts', 'mp'), 'split'), parts along dimension 0
- losses: float32 [4], P('parts'), parts along dimension 0
The draws below stay inside these ranges and needn't reach their ends.
There are 2 independent parts, one for each index of `parts`. The reference program is written for one: setup_inputs(seed, part) draws one part's arguments, and reference() takes and returns one part's arrays. A program takes and returns all parts, laid end to end along the dimension named above; each array names one. Nothing has to cross between parts.
All inputs are finite; a program needn't handle non-finite values.
Results may differ from the reference program's by a relative error of at most 0.0065.
Values may be sent and summed in bfloat16 or wider, within the bound.
A program may use at most 128 MiB of HBM per device.

```python
import jax
import jax.numpy as jnp
from jax import lax

D = 5120
FT = 13824
FA = 6912
FB = 5632
LEN = 64
TOKENS = 192
SEQS = 3


def levels(key, extent, pieces, least, high):
    level = 1.0
    for axis_at, shards_of in pieces:
        draws = jax.random.uniform(jax.random.fold_in(jax.random.fold_in(key, 6), axis_at), (shards_of,), jnp.float32, least / len(pieces), high / len(pieces))
        level = level * jnp.repeat(jnp.exp(draws), extent[axis_at] // shards_of).reshape((-1,) + (1,) * (len(extent) - 1 - axis_at))
    return level


def normal_values(rng, shape, deviation, most, pieces=(), kind=jnp.bfloat16):
    drawn = deviation * jax.random.normal(rng, shape, jnp.float32)
    if pieces:
        drawn = drawn * levels(rng, shape, pieces, -0.22, 0.18)
    return jnp.clip(drawn, -most, most).astype(kind)


def setup_inputs(seed: int = 0, part: int = 0) -> dict:
    key_of = jax.random.split(jax.random.key(seed), 12)
    part_keys = jax.random.split(jax.random.fold_in(key_of[11], part), 12)
    return {
        "tokens": normal_values(part_keys[0], (TOKENS, D), 1.0, 6.0, ((0, 4), (1, 4))),
        "lengths": jax.random.randint(part_keys[1], (SEQS,), 1, LEN + 1).astype(jnp.int32),
        "teacher_gate": normal_values(part_keys[2], (D, FT), D ** -0.5, 0.078125, ((0, 4), (1, 4))),
        "teacher_up": normal_values(part_keys[3], (D, FT), D ** -0.5, 0.078125, ((0, 4), (1, 4))),
        "teacher_down": normal_values(part_keys[4], (FT, D), FT ** -0.5, 0.0546875, ((0, 4), (1, 4))),
        "first_gate": normal_values(part_keys[5], (D, FA), D ** -0.5, 0.078125, ((0, 4), (1, 4))),
        "first_up": normal_values(part_keys[6], (D, FA), D ** -0.5, 0.078125, ((0, 4), (1, 4))),
        "first_down": normal_values(part_keys[7], (FA, D), FA ** -0.5, 0.078125, ((0, 4), (1, 4))),
        "second_gate": normal_values(part_keys[8], (D, FB), D ** -0.5, 0.078125, ((0, 4), (1, 4))),
        "second_up": normal_values(part_keys[9], (D, FB), D ** -0.5, 0.078125, ((0, 4), (1, 4))),
        "second_down": normal_values(part_keys[10], (FB, D), FB ** -0.5, 0.078125, ((0, 4), (1, 4))),
    }


def contract_rows(left, right):
    return lax.dot_general(left, right, (((0,), (0,)), ((), ())), preferred_element_type=jnp.float32)


def reference(tokens, lengths, teacher_gate, teacher_up, teacher_down, first_gate, first_up, first_down, second_gate, second_up, second_down):
    def forward(gate_w, up_w):
        gate = jnp.dot(tokens, gate_w, preferred_element_type=jnp.float32)
        up = jnp.dot(tokens, up_w, preferred_element_type=jnp.float32)
        return gate, up, (jax.nn.silu(gate) * up).astype(jnp.bfloat16)

    _, _, hidden_teacher = forward(teacher_gate, teacher_up)
    gate_first, up_first, hidden_first = forward(first_gate, first_up)
    gate_second, up_second, hidden_second = forward(second_gate, second_up)
    target = jnp.dot(hidden_teacher, teacher_down, preferred_element_type=jnp.float32)
    diff_first = jnp.dot(hidden_first, first_down, preferred_element_type=jnp.float32) - target
    diff_second = jnp.dot(hidden_second, second_down, preferred_element_type=jnp.float32) - target
    position = jnp.arange(TOKENS, dtype=jnp.int32)
    seq_ids = position // LEN
    within = position - seq_ids * LEN
    limit = jnp.sum(jnp.where(seq_ids[:, None] == jnp.arange(SEQS, dtype=jnp.int32)[None, :], lengths[None, :], 0), axis=1)
    mask = (within < limit).astype(jnp.float32)[:, None]
    counted = jnp.sum(lengths).astype(jnp.float32)
    loss_first = jnp.sum(mask * diff_first * diff_first) / counted
    loss_second = jnp.sum(mask * diff_second * diff_second) / counted

    def backward(diff, gate, up, hidden, gate_w, down_w):
        cotangent = (2.0 * mask * diff / counted).astype(jnp.bfloat16)
        grad_down = contract_rows(hidden, cotangent).astype(jnp.bfloat16)
        back = lax.dot_general(cotangent, down_w, (((1,), (1,)), ((), ())), preferred_element_type=jnp.float32)
        sig = jax.nn.sigmoid(gate)
        dgate = (back * up * sig * (1.0 + gate * (1.0 - sig))).astype(jnp.bfloat16)
        dup = (back * gate * sig).astype(jnp.bfloat16)
        return contract_rows(tokens, dgate).astype(jnp.bfloat16), contract_rows(tokens, dup).astype(jnp.bfloat16), grad_down

    first_g, first_u, first_d = backward(diff_first, gate_first, up_first, hidden_first, first_gate, first_down)
    second_g, second_u, second_d = backward(diff_second, gate_second, up_second, hidden_second, second_gate, second_down)
    return first_g, first_u, first_d, second_g, second_u, second_d, jnp.stack([loss_first, loss_second])
```

```python
import functools

import jax
import jax.numpy as jnp
from jax import lax
from jax.experimental import pallas as pl
from jax.experimental.pallas import tpu as pltpu
from jax.sharding import PartitionSpec as P

MESH = pl.DeviceIdType.MESH
VMEM = pl.BlockSpec(memory_space=pltpu.VMEM)
ANY = pl.BlockSpec(memory_space=pl.ANY)
TILE = 384
GRANT = 60 * 2**20

LEN = 64


def contract_rows(left, right):
    return lax.dot_general(
        left, right, (((0,), (0,)), ((), ())), preferred_element_type=jnp.float32
    )


def valid_rows(lengths, count):
    position = jnp.arange(count, dtype=jnp.int32)
    seq_ids = position // LEN
    within = position - seq_ids * LEN
    limit = jnp.sum(
        jnp.where(
            seq_ids[:, None] == jnp.arange(lengths.shape[0], dtype=jnp.int32)[None, :],
            lengths[None, :],
            0,
        ),
        axis=1,
    )
    return (within < limit).astype(jnp.float32)[:, None]


def activate(gate, up):
    return (jax.nn.silu(gate) * up).astype(jnp.bfloat16)


def hidden_grads(back, gate, up):
    sig = jax.nn.sigmoid(gate)
    dgate = (back * up * sig * (1.0 + gate * (1.0 - sig))).astype(jnp.bfloat16)
    dup = (back * gate * sig).astype(jnp.bfloat16)
    return (dgate, dup)


class Links:
    def __init__(self, send, recv):
        self.send, self.recv, self.made = send, recv, []

    def copy(self, src, dst, device):
        at = len(self.made)
        made = pltpu.make_async_remote_copy(
            src_ref=src,
            dst_ref=dst,
            send_sem=self.send.at[at],
            recv_sem=self.recv.at[at],
            device_id=device,
            device_id_type=MESH,
        )
        made.start()
        self.made.append(made)
        return made

    def drain(self):
        for made in self.made:
            made.wait_send()


def greet(devices):
    barrier = pltpu.get_barrier_semaphore()
    for device in devices:
        pl.semaphore_signal(barrier, inc=1, device_id=device, device_id_type=MESH)
    pl.semaphore_wait(barrier, len(devices))


def tiles(width, body):
    full = width // TILE
    if full:

        @pl.loop(0, full)
        def _(i):
            body(pl.ds(pl.multiple_of(i * TILE, 128), TILE))

    if width % TILE:
        body(pl.ds(full * TILE, width % TILE))


def split_places():
    me = lax.axis_index("split")
    chip, core = me // 2, me % 2
    sib = chip * 2 + (1 - core)
    far = (1 - chip) * 2 + core
    diag = (1 - chip) * 2 + (1 - core)
    return me, sib, far, diag


def rows_at(block, count):
    return pl.ds(pl.multiple_of(block * count, 16), count)


class Unit:
    def __init__(self, links, sib, far, refs):
        self.links, self.sib, self.far = links, sib, far
        self.snd1, self.own, self.rcv1, self.snd2, self.rcv2 = refs
        self.half = self.snd1.shape[0] // 2
        self.width = self.snd1.shape[1]

    def multiply(self, left, weight, transposed):
        def body(cols):
            if transposed:
                right, dims = weight[cols, :], (((1,), (1,)), ((), ()))
            else:
                right, dims = weight[:, cols], (((1,), (0,)), ((), ()))
            out = lax.dot_general(left[...], right, dims, preferred_element_type=jnp.float32)
            pair = 2 * self.half
            self.snd1[:, cols] = out[:pair].astype(jnp.bfloat16)
            self.own[:, cols] = out[pair:]

        tiles(self.width, body)
        self.first = self.links.copy(self.snd1, self.rcv1, {"split": self.sib})

    def forward(self):
        self.first.wait_recv()
        half = self.half

        def body(cols):
            both = self.own[:half, cols] + self.rcv1[:half, cols].astype(jnp.float32)
            self.snd2[:, cols] = both.astype(jnp.bfloat16)

        tiles(self.width, body)
        self.second = self.links.copy(self.snd2, self.rcv2, {"split": self.far})

    def ready(self):
        self.second.wait_recv()

    def value(self, cols):
        half = self.half
        return (
            self.own[half:, cols]
            + self.rcv1[half:, cols].astype(jnp.float32)
            + self.rcv2[:, cols].astype(jnp.float32)
        )


def unit_scratch(rows, width):
    half, pair = rows // 4, rows // 2
    return [
        pltpu.VMEM((pair, width), jnp.bfloat16),
        pltpu.VMEM((pair, width), jnp.float32),
        pltpu.VMEM((pair, width), jnp.bfloat16),
        pltpu.VMEM((half, width), jnp.bfloat16),
        pltpu.VMEM((half, width), jnp.bfloat16),
    ]


class Spread:
    def __init__(self, links, ref, count, me, sib, far):
        self.links, self.ref, self.count, self.sib, self.far_at = links, ref, count, sib, far
        mine = ref.at[rows_at(me, count)]
        self.out = links.copy(mine, mine, {"split": far})
        self.side = links.copy(mine, mine, {"split": sib})

    def relay(self):
        self.out.wait_recv()
        theirs = self.ref.at[rows_at(self.far_at, self.count)]
        self.last = self.links.copy(theirs, theirs, {"split": self.sib})

    def finish(self):
        self.side.wait_recv()
        self.last.wait_recv()


def arrange(dst, src, order, count):
    for i, block in enumerate(order):
        dst[i * count : (i + 1) * count, :] = src[rows_at(block, count), :]


def forward_kernel(mp, flips, *refs):
    tok, weights = refs[0], refs[1:7]
    gathered, hidden, kept = refs[7], refs[8:11], refs[11:15]
    xp, wbuf = refs[15], refs[16:22]
    send, recv, wsem = refs[-3:]
    scratch = refs[22:-3]
    loads = [pltpu.make_async_copy(weights[i], wbuf[i], wsem.at[i]) for i in range(6)]
    for load in loads:
        load.start()
    me, sib, far, diag = split_places()
    z = lax.axis_index("mp")
    peers = [{"mp": (z + k) % mp} for k in range(1, mp)]
    greet(peers + [{"split": sib}, {"split": far}])
    links = Links(send, recv)
    block = tok.shape[0]
    count = gathered.shape[0] // 4
    moves = [links.copy(tok, gathered.at[rows_at(z, block)], peer) for peer in peers]
    gathered[rows_at(z, block), :] = tok[...]
    for move in moves:
        move.wait_recv()
    arrange(xp, gathered, (diag, sib, far, me), count)
    units = [Unit(links, sib, far, scratch[5 * i : 5 * i + 5]) for i in range(6)]

    def multiply(i):
        loads[i].wait()
        units[i].multiply(xp, wbuf[i], flips[i])

    spreads = [None] * 3

    def activate_rows(layer):
        gate, up = units[2 * layer], units[2 * layer + 1]
        gate.ready()
        up.ready()
        out = hidden[layer]

        def body(cols):
            g, u = gate.value(cols), up.value(cols)
            out[rows_at(me, count), cols] = (g * jax.nn.sigmoid(g) * u).astype(jnp.bfloat16)
            if layer < 2:
                kept[2 * layer][:, cols] = g
                kept[2 * layer + 1][:, cols] = u

        tiles(gate.width, body)
        spreads[layer] = Spread(links, out, count, me, sib, far)

    multiply(0)
    multiply(1)
    units[0].forward()
    multiply(2)
    units[1].forward()
    multiply(3)
    units[2].forward()
    units[3].forward()
    multiply(4)
    units[4].forward()
    activate_rows(0)
    multiply(5)
    units[5].forward()
    activate_rows(1)
    spreads[0].relay()
    spreads[1].relay()
    activate_rows(2)
    spreads[2].relay()
    for spread in spreads:
        spread.finish()
    links.drain()


def forward_call(mp, tokens, weights, flips):
    block, depth = tokens.shape
    rows = block * mp
    count = rows // 4
    widths = [w.shape[0] if flip else w.shape[1] for w, flip in zip(weights, flips)]
    shape = jax.ShapeDtypeStruct
    outs = [shape((rows, depth), jnp.bfloat16)]
    outs += [shape((rows, widths[2 * i]), jnp.bfloat16) for i in range(3)]
    outs += [shape((count, widths[i]), jnp.float32) for i in range(4)]
    scratch = [pltpu.VMEM((rows, depth), jnp.bfloat16)]
    scratch += [pltpu.VMEM(w.shape, jnp.bfloat16) for w in weights]
    for width in widths:
        scratch += unit_scratch(rows, width)
    copies = (mp - 1) + 2 * 6 + 3 * 3
    scratch += [pltpu.SemaphoreType.DMA((copies,))] * 2 + [pltpu.SemaphoreType.DMA((6,))]
    return pl.pallas_call(
        functools.partial(forward_kernel, mp, flips),
        out_shape=outs,
        in_specs=[VMEM] + [ANY] * 6,
        out_specs=[VMEM] * 8,
        scratch_shapes=scratch,
        compiler_params=pltpu.CompilerParams(
            collective_id=0, has_side_effects=True, vmem_limit_bytes=GRANT
        ),
    )(tokens, *weights)


def cotangent_kernel(mp, *refs):
    diffs, scale = refs[0:2], refs[2]
    cots, loss = refs[3:5], refs[5]
    snds, rcvs = refs[6:8], refs[8:10]
    part, send, recv = refs[10:]
    z = lax.axis_index("mp")
    places = [(z + k) % mp for k in range(1, mp)]
    greet([{"mp": place} for place in places])
    links = Links(send, recv)
    block = scale.shape[0] // mp
    mine = rows_at(z, block)
    moves = []
    for diff, snd, rcv in zip(diffs, snds, rcvs):
        snd[...] = diff[...].astype(jnp.bfloat16)
        moves.append(
            [
                links.copy(snd.at[rows_at(place, block)], rcv.at[k], {"mp": place})
                for k, place in enumerate(places)
            ]
        )
    factor = scale[mine, 0:1]
    spread, sums = [], []
    for diff, rcv, cot, made in zip(diffs, rcvs, cots, moves):
        total = diff[mine, :]
        for k, move in enumerate(made):
            move.wait_recv()
            total = total + rcv[k].astype(jnp.float32)
        scaled = factor * total
        cot[mine, :] = scaled.astype(jnp.bfloat16)
        sums.append(0.5 * jnp.sum(scaled * total, keepdims=True))
        own = cot.at[mine]
        spread += [links.copy(own, own, {"mp": place}) for place in places]
    row = lax.broadcasted_iota(jnp.int32, part.shape[1:], 0)
    part[0] = jnp.where(row == 0, sums[0], sums[1])
    spread += [links.copy(part.at[0], part.at[k + 1], {"mp": p}) for k, p in enumerate(places)]
    for move in spread:
        move.wait_recv()
    whole = part[0]
    for k in range(1, mp):
        whole = whole + part[k]
    loss[...] = whole
    links.drain()


def cotangent_call(mp, diffs, scale):
    rows, width = diffs[0].shape
    block = rows // mp
    shape = jax.ShapeDtypeStruct
    return pl.pallas_call(
        functools.partial(cotangent_kernel, mp),
        out_shape=[shape((rows, width), jnp.bfloat16)] * 2 + [shape((8, 128), jnp.float32)],
        in_specs=[VMEM] * 3,
        out_specs=[VMEM] * 3,
        scratch_shapes=[pltpu.VMEM((rows, width), jnp.bfloat16)] * 2
        + [pltpu.VMEM((mp - 1, block, width), jnp.bfloat16)] * 2
        + [pltpu.VMEM((mp, 8, 128), jnp.float32)]
        + [pltpu.SemaphoreType.DMA((5 * (mp - 1),))] * 2,
        compiler_params=pltpu.CompilerParams(
            collective_id=1, has_side_effects=True, vmem_limit_bytes=GRANT
        ),
    )(*diffs, scale)


def backward_kernel(*refs):
    cots, downs, kept, part_in = refs[0:2], refs[2:4], refs[4:8], refs[8]
    grads, loss = refs[9:13], refs[13]
    xps, wbuf, part = refs[14:16], refs[16:18], refs[18]
    send, recv, wsem = refs[-3:]
    scratch = refs[19:-3]
    loads = [pltpu.make_async_copy(downs[i], wbuf[i], wsem.at[i]) for i in range(2)]
    for load in loads:
        load.start()
    me, sib, far, diag = split_places()
    greet([{"split": place} for place in (sib, far, diag)])
    links = Links(send, recv)
    count = cots[0].shape[0] // 4
    units = [Unit(links, sib, far, scratch[5 * i : 5 * i + 5]) for i in range(2)]
    for i in range(2):
        arrange(xps[i], cots[i], (diag, sib, far, me), count)
        loads[i].wait()
        units[i].multiply(xps[i], wbuf[i], True)
    part[0] = part_in[...]
    marks = [
        links.copy(part.at[0], part.at[k + 1], {"split": place})
        for k, place in enumerate((sib, far, diag))
    ]
    units[0].forward()
    units[1].forward()
    spreads = []
    for i in range(2):
        units[i].ready()

        def body(cols, i=i):
            back = units[i].value(cols)
            gate, up = kept[2 * i][:, cols], kept[2 * i + 1][:, cols]
            sig = jax.nn.sigmoid(gate)
            dgate = back * up * sig * (1.0 + gate * (1.0 - sig))
            grads[2 * i][rows_at(me, count), cols] = dgate.astype(jnp.bfloat16)
            grads[2 * i + 1][rows_at(me, count), cols] = (back * gate * sig).astype(jnp.bfloat16)

        tiles(units[i].width, body)
        spreads += [Spread(links, grads[2 * i + j], count, me, sib, far) for j in range(2)]
    for mark in marks:
        mark.wait_recv()
    loss[...] = part[0] + part[1] + part[2] + part[3]
    for spread in spreads:
        spread.relay()
    for spread in spreads:
        spread.finish()
    links.drain()


def backward_call(cots, downs, kept, part):
    rows, width = cots[0].shape
    widths = [down.shape[0] for down in downs]
    shape = jax.ShapeDtypeStruct
    outs = [shape((rows, widths[i // 2]), jnp.bfloat16) for i in range(4)]
    outs.append(shape((8, 128), jnp.float32))
    scratch = [pltpu.VMEM((rows, width), jnp.bfloat16)] * 2
    scratch += [pltpu.VMEM(down.shape, jnp.bfloat16) for down in downs]
    scratch += [pltpu.VMEM((4, 8, 128), jnp.float32)]
    for w in widths:
        scratch += unit_scratch(rows, w)
    copies = 2 * 2 + 3 * 4 + 3
    scratch += [pltpu.SemaphoreType.DMA((copies,))] * 2 + [pltpu.SemaphoreType.DMA((2,))]
    return pl.pallas_call(
        backward_kernel,
        out_shape=outs,
        in_specs=[VMEM] * 2 + [ANY] * 2 + [VMEM] * 5,
        out_specs=[VMEM] * 5,
        scratch_shapes=scratch,
        compiler_params=pltpu.CompilerParams(
            collective_id=2, has_side_effects=True, vmem_limit_bytes=GRANT
        ),
    )(*cots, *downs, *kept, part)


def per_device_kernels(
    mp,
    tokens,
    lengths,
    teacher_gate,
    teacher_up,
    teacher_down,
    first_gate,
    first_up,
    first_down,
    second_gate,
    second_up,
    second_down,
):
    weights, flips = [], []
    for w in (first_gate, first_up, second_gate, second_up, teacher_gate, teacher_up):
        flip = w.shape[1] % 128 != 0
        flips.append(flip)
        weights.append(w.T if flip else w)
    gathered, *rest = forward_call(mp, tokens, weights, tuple(flips))
    hidden, kept = rest[:3], rest[3:]
    target = jnp.dot(hidden[2], teacher_down, preferred_element_type=jnp.float32)
    diffs = (
        jnp.dot(hidden[0], first_down, preferred_element_type=jnp.float32) - target,
        jnp.dot(hidden[1], second_down, preferred_element_type=jnp.float32) - target,
    )
    counted = jnp.sum(lengths).astype(jnp.float32)
    mask = valid_rows(lengths, gathered.shape[0])
    scale = jnp.broadcast_to(2.0 * mask / counted, (mask.shape[0], 128))
    *cots, part = cotangent_call(mp, diffs, scale)
    *grads_in, loss = backward_call(cots, (first_down, second_down), kept, part)
    downs = [contract_rows(hidden[i], cots[i]).astype(jnp.bfloat16) for i in range(2)]
    outs = []
    for item, flip in zip(grads_in, flips):
        if flip:
            outs.append(contract_rows(item, gathered).astype(jnp.bfloat16).T)
        else:
            outs.append(contract_rows(gathered, item).astype(jnp.bfloat16))
    return outs[0], outs[1], downs[0], outs[2], outs[3], downs[1], loss[0:2, 0]


def per_device(
    tokens,
    lengths,
    teacher_gate,
    teacher_up,
    teacher_down,
    first_gate,
    first_up,
    first_down,
    second_gate,
    second_up,
    second_down,
):
    gathered = lax.all_gather(tokens, "mp", axis=0, tiled=True)
    total_rows = gathered.shape[0]

    def project(weight):
        return jnp.dot(gathered, weight, preferred_element_type=jnp.float32)

    partials = (
        project(teacher_gate),
        project(teacher_up),
        project(first_gate),
        project(first_up),
        project(second_gate),
        project(second_up),
    )
    values = lax.psum(
        (partials[0], partials[1], partials[2], partials[3], partials[4], partials[5]), "split"
    )
    hidden = (
        activate(values[0], values[1]),
        activate(values[2], values[3]),
        activate(values[4], values[5]),
    )
    target = jnp.dot(hidden[0], teacher_down, preferred_element_type=jnp.float32)
    diffs = (
        jnp.dot(hidden[1], first_down, preferred_element_type=jnp.float32) - target,
        jnp.dot(hidden[2], second_down, preferred_element_type=jnp.float32) - target,
    )
    counted = jnp.sum(lengths).astype(jnp.float32)
    summed = lax.psum((diffs[0], diffs[1]), "mp")
    mask = valid_rows(lengths, total_rows)
    partial_loss = (
        jnp.stack([jnp.sum(mask * summed[0] * summed[0]), jnp.sum(mask * summed[1] * summed[1])])
        / counted
    )
    losses = lax.psum(partial_loss, "split")
    cotangents = (
        (2.0 * mask * summed[0] / counted).astype(jnp.bfloat16),
        (2.0 * mask * summed[1] / counted).astype(jnp.bfloat16),
    )
    grad_first_down = contract_rows(hidden[1], cotangents[0]).astype(jnp.bfloat16)
    grad_second_down = contract_rows(hidden[2], cotangents[1]).astype(jnp.bfloat16)
    dims = (((1,), (1,)), ((), ()))
    backs = (
        lax.dot_general(cotangents[0], first_down, dims, preferred_element_type=jnp.float32),
        lax.dot_general(cotangents[1], second_down, dims, preferred_element_type=jnp.float32),
    )
    back_full = lax.psum((backs[0], backs[1]), "split")
    first_dg, first_du = hidden_grads(back_full[0], values[2], values[3])
    second_dg, second_du = hidden_grads(back_full[1], values[4], values[5])
    grads_in = (first_dg, first_du, second_dg, second_du)
    outputs = tuple((contract_rows(gathered, item).astype(jnp.bfloat16) for item in grads_in))
    return (
        outputs[0],
        outputs[1],
        grad_first_down,
        outputs[2],
        outputs[3],
        grad_second_down,
        losses,
    )


def run(mp, split, *args):
    rows = args[0].shape[0] * mp
    if split == 4 and mp > 1 and args[0].shape[0] % 16 == 0 and rows % 64 == 0:
        return per_device_kernels(mp, *args)
    return per_device(*args)


def solution(mesh):
    placed = (
        P(("parts", "mp"), "split"),
        P("parts"),
        P(("parts", "split"), "mp"),
        P(("parts", "split"), "mp"),
        P(("parts", "mp"), "split"),
        P(("parts", "split"), "mp"),
        P(("parts", "split"), "mp"),
        P(("parts", "mp"), "split"),
        P(("parts", "split"), "mp"),
        P(("parts", "split"), "mp"),
        P(("parts", "mp"), "split"),
    )
    return jax.shard_map(
        functools.partial(run, mesh.shape["mp"], mesh.shape["split"]),
        mesh=mesh,
        in_specs=placed,
        out_specs=(
            P(("parts", "split"), "mp"),
            P(("parts", "split"), "mp"),
            P(("parts", "mp"), "split"),
            P(("parts", "split"), "mp"),
            P(("parts", "split"), "mp"),
            P(("parts", "mp"), "split"),
            P("parts"),
        ),
        check_vma=False,
    )
```

```python
import functools

import jax
import jax.numpy as jnp
from jax import lax
from jax.experimental import pallas as pl
from jax.experimental.pallas import tpu as pltpu
from jax.sharding import PartitionSpec as P

MESH = pl.DeviceIdType.MESH
VMEM = pl.BlockSpec(memory_space=pltpu.VMEM)
ANY = pl.BlockSpec(memory_space=pl.ANY)
TILE = 384
GRANT = 60 * 2**20

LEN = 64


def contract_rows(left, right):
    return lax.dot_general(
        left, right, (((0,), (0,)), ((), ())), preferred_element_type=jnp.float32
    )


def valid_rows(lengths, count):
    position = jnp.arange(count, dtype=jnp.int32)
    seq_ids = position // LEN
    within = position - seq_ids * LEN
    limit = jnp.sum(
        jnp.where(
            seq_ids[:, None] == jnp.arange(lengths.shape[0], dtype=jnp.int32)[None, :],
            lengths[None, :],
            0,
        ),
        axis=1,
    )
    return (within < limit).astype(jnp.float32)[:, None]


def activate(gate, up):
    return (jax.nn.silu(gate) * up).astype(jnp.bfloat16)


def hidden_grads(back, gate, up):
    sig = jax.nn.sigmoid(gate)
    dgate = (back * up * sig * (1.0 + gate * (1.0 - sig))).astype(jnp.bfloat16)
    dup = (back * gate * sig).astype(jnp.bfloat16)
    return (dgate, dup)


class Links:
    def __init__(self, send, recv):
        self.send, self.recv, self.made = send, recv, []

    def copy(self, src, dst, device):
        at = len(self.made)
        made = pltpu.make_async_remote_copy(
            src_ref=src,
            dst_ref=dst,
            send_sem=self.send.at[at],
            recv_sem=self.recv.at[at],
            device_id=device,
            device_id_type=MESH,
        )
        made.start()
        self.made.append(made)
        return made

    def drain(self):
        for made in self.made:
            made.wait_send()


def greet(devices):
    barrier = pltpu.get_barrier_semaphore()
    for device in devices:
        pl.semaphore_signal(barrier, inc=1, device_id=device, device_id_type=MESH)
    pl.semaphore_wait(barrier, len(devices))


def tiles(width, body):
    full = width // TILE
    if full:

        @pl.loop(0, full)
        def _(i):
            body(pl.ds(pl.multiple_of(i * TILE, 128), TILE))

    if width % TILE:
        body(pl.ds(full * TILE, width % TILE))


def four_places(axis):
    me = lax.axis_index(axis)
    chip, core = me // 2, me % 2
    sib = chip * 2 + (1 - core)
    far = (1 - chip) * 2 + core
    diag = (1 - chip) * 2 + (1 - core)
    return me, sib, far, diag


def rows_at(block, count):
    return pl.ds(pl.multiple_of(block * count, 16), count)


class Unit:
    def __init__(self, links, sib, far, refs):
        self.links, self.sib, self.far = links, sib, far
        self.snd1, self.own, self.rcv1, self.snd2, self.rcv2 = refs
        self.half = self.snd1.shape[0] // 2
        self.width = self.snd1.shape[1]

    def multiply(self, left, weight, transposed):
        def body(cols):
            if transposed:
                right, dims = weight[cols, :], (((1,), (1,)), ((), ()))
            else:
                right, dims = weight[:, cols], (((1,), (0,)), ((), ()))
            out = lax.dot_general(left[...], right, dims, preferred_element_type=jnp.float32)
            pair = 2 * self.half
            self.snd1[:, cols] = out[:pair].astype(jnp.bfloat16)
            self.own[:, cols] = out[pair:]

        tiles(self.width, body)
        self.first = self.links.copy(self.snd1, self.rcv1, {"split": self.sib})

    def forward(self):
        self.first.wait_recv()
        half = self.half

        def body(cols):
            both = self.own[:half, cols] + self.rcv1[:half, cols].astype(jnp.float32)
            self.snd2[:, cols] = both.astype(jnp.bfloat16)

        tiles(self.width, body)
        self.second = self.links.copy(self.snd2, self.rcv2, {"split": self.far})

    def ready(self):
        self.second.wait_recv()

    def value(self, cols):
        half = self.half
        return (
            self.own[half:, cols]
            + self.rcv1[half:, cols].astype(jnp.float32)
            + self.rcv2[:, cols].astype(jnp.float32)
        )


def unit_scratch(rows, width):
    half, pair = rows // 4, rows // 2
    return [
        pltpu.VMEM((pair, width), jnp.bfloat16),
        pltpu.VMEM((pair, width), jnp.float32),
        pltpu.VMEM((pair, width), jnp.bfloat16),
        pltpu.VMEM((half, width), jnp.bfloat16),
        pltpu.VMEM((half, width), jnp.bfloat16),
    ]


class Spread:
    def __init__(self, links, ref, count, places, axis="split", source=None):
        me, self.sib, self.far = places[:3]
        self.links, self.ref, self.count, self.axis = links, ref, count, axis
        mine = ref.at[rows_at(me, count)]
        source = mine if source is None else source
        self.out = links.copy(source, mine, {axis: self.far})
        self.side = links.copy(source, mine, {axis: self.sib})

    def relay(self):
        self.out.wait_recv()
        theirs = self.ref.at[rows_at(self.far, self.count)]
        self.last = self.links.copy(theirs, theirs, {self.axis: self.sib})

    def finish(self):
        self.side.wait_recv()
        self.last.wait_recv()


def arrange(dst, src, order, count):
    for i, block in enumerate(order):
        dst[i * count : (i + 1) * count, :] = src[rows_at(block, count), :]


def forward_kernel(flips, *refs):
    tok, weights = refs[0], refs[1:7]
    gathered, hidden, kept = refs[7], refs[8:11], refs[11:15]
    xp, wbuf = refs[15], refs[16:22]
    send, recv, wsem = refs[-3:]
    scratch = refs[22:-3]
    loads = [pltpu.make_async_copy(weights[i], wbuf[i], wsem.at[i]) for i in range(6)]
    for load in loads:
        load.start()
    places, ring = four_places("split"), four_places("mp")
    me, sib, far, diag = places
    greet([{"split": p} for p in (sib, far)] + [{"mp": p} for p in ring[1:3]])
    links = Links(send, recv)
    block = tok.shape[0]
    count = gathered.shape[0] // 4
    moves = Spread(links, gathered, block, ring, "mp", tok)
    gathered[rows_at(ring[0], block), :] = tok[...]
    moves.relay()
    moves.finish()
    arrange(xp, gathered, (diag, sib, far, me), count)
    units = [Unit(links, sib, far, scratch[5 * i : 5 * i + 5]) for i in range(6)]

    def multiply(i):
        loads[i].wait()
        units[i].multiply(xp, wbuf[i], flips[i])

    spreads = [None] * 3

    def activate_rows(layer):
        gate, up = units[2 * layer], units[2 * layer + 1]
        gate.ready()
        up.ready()
        out = hidden[layer]

        def body(cols):
            g, u = gate.value(cols), up.value(cols)
            out[rows_at(me, count), cols] = (g * jax.nn.sigmoid(g) * u).astype(jnp.bfloat16)
            if layer < 2:
                kept[2 * layer][:, cols] = g
                kept[2 * layer + 1][:, cols] = u

        tiles(gate.width, body)
        spreads[layer] = Spread(links, out, count, places)

    multiply(0)
    multiply(1)
    units[0].forward()
    multiply(2)
    units[1].forward()
    multiply(3)
    units[2].forward()
    units[3].forward()
    multiply(4)
    units[4].forward()
    activate_rows(0)
    multiply(5)
    units[5].forward()
    activate_rows(1)
    spreads[0].relay()
    spreads[1].relay()
    activate_rows(2)
    spreads[2].relay()
    for spread in spreads:
        spread.finish()
    links.drain()


def forward_call(mp, tokens, weights, flips):
    block, depth = tokens.shape
    rows = block * mp
    count = rows // 4
    widths = [w.shape[0] if flip else w.shape[1] for w, flip in zip(weights, flips)]
    shape = jax.ShapeDtypeStruct
    outs = [shape((rows, depth), jnp.bfloat16)]
    outs += [shape((rows, widths[2 * i]), jnp.bfloat16) for i in range(3)]
    outs += [shape((count, widths[i]), jnp.float32) for i in range(4)]
    scratch = [pltpu.VMEM((rows, depth), jnp.bfloat16)]
    scratch += [pltpu.VMEM(w.shape, jnp.bfloat16) for w in weights]
    for width in widths:
        scratch += unit_scratch(rows, width)
    copies = 3 + 2 * 6 + 3 * 3
    scratch += [pltpu.SemaphoreType.DMA((copies,))] * 2 + [pltpu.SemaphoreType.DMA((6,))]
    return pl.pallas_call(
        functools.partial(forward_kernel, flips),
        out_shape=outs,
        in_specs=[VMEM] + [ANY] * 6,
        out_specs=[VMEM] * 8,
        scratch_shapes=scratch,
        compiler_params=pltpu.CompilerParams(
            collective_id=0, has_side_effects=True, vmem_limit_bytes=GRANT
        ),
    )(tokens, *weights)


def backward_kernel(*refs):
    diffs, scale, downs, kept = refs[0:2], refs[2], refs[3:5], refs[5:9]
    cots, grads, loss = refs[9:11], refs[11:15], refs[15]
    snds, rcvs, xps, wbuf = refs[16:18], refs[18:20], refs[20:22], refs[22:24]
    part, marked = refs[24:26]
    send, recv, wsem = refs[-3:]
    scratch = refs[26:-3]
    loads = [pltpu.make_async_copy(downs[i], wbuf[i], wsem.at[i]) for i in range(2)]
    for load in loads:
        load.start()
    places, ring = four_places("split"), four_places("mp")
    me, sib, far, diag = places
    greet([{"mp": p} for p in ring[1:]] + [{"split": p} for p in places[1:]])
    links = Links(send, recv)
    block = count = scale.shape[0] // 4
    mine = rows_at(ring[0], block)
    moves = []
    for diff, snd, rcv in zip(diffs, snds, rcvs):
        snd[...] = diff[...].astype(jnp.bfloat16)
        moves.append(
            [
                links.copy(snd.at[rows_at(p, block)], rcv.at[k], {"mp": p})
                for k, p in enumerate(ring[1:])
            ]
        )
    factor = scale[mine, 0:1]
    units = [Unit(links, sib, far, scratch[5 * i : 5 * i + 5]) for i in range(2)]
    turns, sums = [], []
    for diff, rcv, cot, made in zip(diffs, rcvs, cots, moves):
        total = diff[mine, :]
        for k, move in enumerate(made):
            move.wait_recv()
            total = total + rcv[k].astype(jnp.float32)
        scaled = factor * total
        cot[mine, :] = scaled.astype(jnp.bfloat16)
        turns.append(Spread(links, cot, block, ring, "mp"))
        sums.append(0.5 * jnp.sum(scaled * total, keepdims=True))
    row = lax.broadcasted_iota(jnp.int32, part.shape[1:], 0)
    part[0] = jnp.where(row == 0, sums[0], sums[1])
    parts = [links.copy(part.at[0], part.at[k], {"mp": ring[k]}) for k in (1, 2, 3)]

    def multiply(i):
        turns[i].finish()
        arrange(xps[i], cots[i], (diag, sib, far, me), count)
        loads[i].wait()
        units[i].multiply(xps[i], wbuf[i], True)

    spreads = []

    def differentiate(i):
        units[i].ready()

        def body(cols):
            back = units[i].value(cols)
            gate, up = kept[2 * i][:, cols], kept[2 * i + 1][:, cols]
            sig = jax.nn.sigmoid(gate)
            dgate = back * up * sig * (1.0 + gate * (1.0 - sig))
            grads[2 * i][rows_at(me, count), cols] = dgate.astype(jnp.bfloat16)
            grads[2 * i + 1][rows_at(me, count), cols] = (back * gate * sig).astype(jnp.bfloat16)

        tiles(units[i].width, body)
        spreads.extend(Spread(links, grads[2 * i + j], count, places) for j in range(2))

    turns[0].relay()
    turns[1].relay()
    multiply(0)
    for move in parts:
        move.wait_recv()
    marked[0] = part[0] + part[1] + part[2] + part[3]
    marks = [links.copy(marked.at[0], marked.at[k], {"split": places[k]}) for k in (1, 2, 3)]
    units[0].forward()
    multiply(1)
    units[1].forward()
    differentiate(0)
    differentiate(1)
    for mark in marks:
        mark.wait_recv()
    loss[...] = marked[0] + marked[1] + marked[2] + marked[3]
    for spread in spreads:
        spread.relay()
    for spread in spreads:
        spread.finish()
    links.drain()


def backward_call(diffs, scale, downs, kept):
    rows, width = diffs[0].shape
    block = rows // 4
    widths = [down.shape[0] for down in downs]
    shape = jax.ShapeDtypeStruct
    outs = [shape((rows, width), jnp.bfloat16)] * 2
    outs += [shape((rows, widths[i // 2]), jnp.bfloat16) for i in range(4)]
    outs.append(shape((8, 128), jnp.float32))
    scratch = [pltpu.VMEM((rows, width), jnp.bfloat16)] * 2
    scratch += [pltpu.VMEM((3, block, width), jnp.bfloat16)] * 2
    scratch += [pltpu.VMEM((rows, width), jnp.bfloat16)] * 2
    scratch += [pltpu.VMEM(down.shape, jnp.bfloat16) for down in downs]
    scratch += [pltpu.VMEM((4, 8, 128), jnp.float32)] * 2
    for w in widths:
        scratch += unit_scratch(rows, w)
    copies = 2 * 3 + 2 * 3 + 3 + 2 * 2 + 3 * 4 + 3
    scratch += [pltpu.SemaphoreType.DMA((copies,))] * 2 + [pltpu.SemaphoreType.DMA((2,))]
    return pl.pallas_call(
        backward_kernel,
        out_shape=outs,
        in_specs=[VMEM] * 3 + [ANY] * 2 + [VMEM] * 4,
        out_specs=[VMEM] * 7,
        scratch_shapes=scratch,
        compiler_params=pltpu.CompilerParams(
            collective_id=1, has_side_effects=True, vmem_limit_bytes=GRANT
        ),
    )(*diffs, scale, *downs, *kept)


def per_device_kernels(
    mp,
    tokens,
    lengths,
    teacher_gate,
    teacher_up,
    teacher_down,
    first_gate,
    first_up,
    first_down,
    second_gate,
    second_up,
    second_down,
):
    weights, flips = [], []
    for w in (first_gate, first_up, second_gate, second_up, teacher_gate, teacher_up):
        flip = w.shape[1] % 128 != 0
        flips.append(flip)
        weights.append(w.T if flip else w)
    gathered, *rest = forward_call(mp, tokens, weights, tuple(flips))
    hidden, kept = rest[:3], rest[3:]
    target = jnp.dot(hidden[2], teacher_down, preferred_element_type=jnp.float32)
    diffs = (
        jnp.dot(hidden[0], first_down, preferred_element_type=jnp.float32) - target,
        jnp.dot(hidden[1], second_down, preferred_element_type=jnp.float32) - target,
    )
    counted = jnp.sum(lengths).astype(jnp.float32)
    mask = valid_rows(lengths, gathered.shape[0])
    scale = jnp.broadcast_to(2.0 * mask / counted, (mask.shape[0], 128))
    *made, loss = backward_call(diffs, scale, (first_down, second_down), kept)
    cots, grads_in = made[:2], made[2:]
    downs = [contract_rows(hidden[i], cots[i]).astype(jnp.bfloat16) for i in range(2)]
    outs = []
    for item, flip in zip(grads_in, flips):
        if flip:
            outs.append(contract_rows(item, gathered).astype(jnp.bfloat16).T)
        else:
            outs.append(contract_rows(gathered, item).astype(jnp.bfloat16))
    return outs[0], outs[1], downs[0], outs[2], outs[3], downs[1], loss[0:2, 0]


def per_device(
    tokens,
    lengths,
    teacher_gate,
    teacher_up,
    teacher_down,
    first_gate,
    first_up,
    first_down,
    second_gate,
    second_up,
    second_down,
):
    gathered = lax.all_gather(tokens, "mp", axis=0, tiled=True)
    total_rows = gathered.shape[0]

    def project(weight):
        return jnp.dot(gathered, weight, preferred_element_type=jnp.float32)

    partials = (
        project(teacher_gate),
        project(teacher_up),
        project(first_gate),
        project(first_up),
        project(second_gate),
        project(second_up),
    )
    values = lax.psum(
        (partials[0], partials[1], partials[2], partials[3], partials[4], partials[5]), "split"
    )
    hidden = (
        activate(values[0], values[1]),
        activate(values[2], values[3]),
        activate(values[4], values[5]),
    )
    target = jnp.dot(hidden[0], teacher_down, preferred_element_type=jnp.float32)
    diffs = (
        jnp.dot(hidden[1], first_down, preferred_element_type=jnp.float32) - target,
        jnp.dot(hidden[2], second_down, preferred_element_type=jnp.float32) - target,
    )
    counted = jnp.sum(lengths).astype(jnp.float32)
    summed = lax.psum((diffs[0], diffs[1]), "mp")
    mask = valid_rows(lengths, total_rows)
    partial_loss = (
        jnp.stack([jnp.sum(mask * summed[0] * summed[0]), jnp.sum(mask * summed[1] * summed[1])])
        / counted
    )
    losses = lax.psum(partial_loss, "split")
    cotangents = (
        (2.0 * mask * summed[0] / counted).astype(jnp.bfloat16),
        (2.0 * mask * summed[1] / counted).astype(jnp.bfloat16),
    )
    grad_first_down = contract_rows(hidden[1], cotangents[0]).astype(jnp.bfloat16)
    grad_second_down = contract_rows(hidden[2], cotangents[1]).astype(jnp.bfloat16)
    dims = (((1,), (1,)), ((), ()))
    backs = (
        lax.dot_general(cotangents[0], first_down, dims, preferred_element_type=jnp.float32),
        lax.dot_general(cotangents[1], second_down, dims, preferred_element_type=jnp.float32),
    )
    back_full = lax.psum((backs[0], backs[1]), "split")
    first_dg, first_du = hidden_grads(back_full[0], values[2], values[3])
    second_dg, second_du = hidden_grads(back_full[1], values[4], values[5])
    grads_in = (first_dg, first_du, second_dg, second_du)
    outputs = tuple((contract_rows(gathered, item).astype(jnp.bfloat16) for item in grads_in))
    return (
        outputs[0],
        outputs[1],
        grad_first_down,
        outputs[2],
        outputs[3],
        grad_second_down,
        losses,
    )


def run(mp, split, *args):
    rows = args[0].shape[0] * mp
    if split == 4 and mp == 4 and args[0].shape[0] % 16 == 0 and rows % 64 == 0:
        return per_device_kernels(mp, *args)
    return per_device(*args)


def solution(mesh):
    placed = (
        P(("parts", "mp"), "split"),
        P("parts"),
        P(("parts", "split"), "mp"),
        P(("parts", "split"), "mp"),
        P(("parts", "mp"), "split"),
        P(("parts", "split"), "mp"),
        P(("parts", "split"), "mp"),
        P(("parts", "mp"), "split"),
        P(("parts", "split"), "mp"),
        P(("parts", "split"), "mp"),
        P(("parts", "mp"), "split"),
    )
    return jax.shard_map(
        functools.partial(run, mesh.shape["mp"], mesh.shape["split"]),
        mesh=mesh,
        in_specs=placed,
        out_specs=(
            P(("parts", "split"), "mp"),
            P(("parts", "split"), "mp"),
            P(("parts", "mp"), "split"),
            P(("parts", "split"), "mp"),
            P(("parts", "split"), "mp"),
            P(("parts", "mp"), "split"),
            P("parts"),
        ),
        check_vma=False,
    )
```
